1024 devices in a mesh: seq: 16 (over z_lo, x), dp: 32 (over y, z_hi), grp: 2 (over core).
Axes of the slice: x: 4, y: 8, z: 16 (z_hi: 4, z_lo: 4; z = z_hi * 4 + z_lo), core: 2. Of those that a mesh axis runs over, the one named last changes fastest.
Arguments:
- video_queries: bfloat16 [32, 2048, 4096], P('dp', 'seq', 'grp'), may hold values from -13.5 to 13.5
- caption_keys: bfloat16 [32, 512, 4096], P('dp', 'seq', 'grp'), may hold values from -6 to 6
- caption_values: bfloat16 [32, 512, 4096], P('dp', 'seq', 'grp'), may hold values from -6 to 6
- out_grad: bfloat16 [32, 2048, 4096], P('dp', 'seq', 'grp'), may hold values from -6 to 6
- head_gate: float32 [32], replicated, may hold values from 0.25 to 2
- video_len: int32 [32], P('dp'), may hold values from 1 to 2048, 32768 in all
- cap_len: int32 [32], P('dp'), may hold values from 1 to 512, 8192 in all
Outputs:
- attended: bfloat16 [32, 2048, 4096], P('dp', 'seq', 'grp')
- query_grad: bfloat16 [32, 2048, 4096], P('dp', 'seq', 'grp')
- key_grad: bfloat16 [32, 512, 4096], P('dp', 'seq', 'grp')
- value_grad: bfloat16 [32, 512, 4096], P('dp', 'seq', 'grp')
- gate_grad: float32 [32], replicated
The draws below stay inside these ranges and needn't reach their ends.
All inputs are finite; a program needn't handle non-finite values. No bound on the sum of `video_len` or of `cap_len` on one device may be relied on, other than what follows from the above.
Results may differ from the reference program's by a relative error of at most 0.017.
Values may be sent and summed in bfloat16 or wider, within the bound.
No kernel may reach another device: no remote copies, remote signals or barrier semaphores. Data moves between devices by JAX's collectives and lax.ppermute only.
A program may use at most 64 MiB of HBM per device.

```python
import math
import jax
import jax.numpy as jnp
import numpy as np
from jax import lax

HEADS = 32
HEAD_DIM = 128
TOK_DEV = 128
CAP = 512
INNER = 4096
SAMPLES = 32
VIDEO = 2048
N_SEQ = 16


def paired_fields(key):
    base = jax.random.fold_in(key, 7001)
    width = HEADS * HEAD_DIM
    cap_keys = jnp.clip(jax.random.normal(jax.random.fold_in(base, 1), (SAMPLES, CAP, width), jnp.float32), -6.0, 6.0)
    queries = jnp.clip(jax.random.normal(jax.random.fold_in(base, 2), (SAMPLES, VIDEO, width), jnp.float32), -6.0, 6.0)
    return (queries, cap_keys)


def draw_video_queries(key, part):
    return paired_fields(key)[0].astype(jnp.bfloat16)


def draw_caption_keys(key, part):
    return paired_fields(key)[1].astype(jnp.bfloat16)


def shard_levels(key, extent, split, smallest, top_value):
    factor_of = 1.0
    for axis_at, shards_of in split:
        draws = jax.random.uniform(jax.random.fold_in(jax.random.fold_in(key, 6), axis_at), (shards_of,), jnp.float32, smallest / len(split), top_value / len(split))
        factor_of = factor_of * jnp.repeat(jnp.exp(draws), extent[axis_at] // shards_of).reshape((-1,) + (1,) * (len(extent) - 1 - axis_at))
    return factor_of


def split_up(amount, total, reach, skew):
    portions = [(1 << 20) // math.isqrt(rank ** skew) + 1 for rank in range(2, amount + 1)]
    spare, given = total - reach - (amount - 1), [1] * (amount - 1)
    while spare > 0:
        candidates = [i for i in range(amount - 1) if given[i] < reach]
        whole, budget = sum([portions[i] for i in candidates]), spare
        for i in candidates:
            more = min(reach - given[i], max(1, budget * portions[i] // whole), spare)
            given[i] = given[i] + more
            spare = spare - more
    return np.array([reach] + given)


def uneven_parts(own_key, amount, total, bound, lean):
    if amount == 2:
        one = jax.random.randint(own_key, (), max(1, total - bound), min(bound, total - 1) + 1)
        return jnp.stack([one, total - one])
    lengths = jnp.asarray(split_up(amount, total, bound, lean), jnp.int32)
    twos = (amount - 1) // 2
    source_of, taker = lengths[1:1 + 2 * twos:2], lengths[2:2 + 2 * twos:2]
    slack = jnp.minimum(source_of - 1, bound - taker)
    moved = jax.random.randint(jax.random.fold_in(own_key, 1), (twos,), 0, 1 << 20) % (slack + 1)
    lengths = lengths.at[1:1 + 2 * twos:2].set(source_of - moved).at[2:2 + 2 * twos:2].set(taker + moved)
    return lengths[jax.random.permutation(jax.random.fold_in(own_key, 2), amount)]


def centred(stream_key, extent, spread, bound, pieces=(), held_as=jnp.bfloat16):
    loudness = shard_levels(stream_key, extent, pieces, -0.22, 0.18) if pieces else 1.0
    values = jax.random.normal(stream_key, extent, jnp.float32) * spread * loudness
    return jnp.minimum(jnp.maximum(values, -bound), bound).astype(held_as)


def setup_inputs(seed: int = 0) -> dict:
    splits = jax.random.split(jax.random.key(seed), 8)
    video_queries = draw_video_queries(jax.random.fold_in(splits[7], 71), 0)
    caption_keys = draw_caption_keys(jax.random.fold_in(splits[7], 71), 0)
    caption_values = centred(splits[2], (SAMPLES, CAP, INNER), 1.0, 6.0, ((0, 32), (1, 16), (2, 2)))
    out_grad = centred(splits[3], (SAMPLES, VIDEO, INNER), 1.0, 6.0, ((0, 32), (1, 16), (2, 2)))
    head_gate = jnp.clip(jnp.exp(jax.random.uniform(splits[4], (HEADS,), jnp.float32, math.log(0.25), math.log(2.0))), 0.25, 2.0)
    video_len = uneven_parts(splits[5], SAMPLES, SAMPLES * VIDEO // 2, VIDEO, 2).astype(jnp.int32)
    cap_len = uneven_parts(splits[6], SAMPLES, SAMPLES * CAP // 2, CAP, 1).astype(jnp.int32)
    return dict(video_queries=video_queries, caption_keys=caption_keys, caption_values=caption_values, out_grad=out_grad, head_gate=head_gate, video_len=video_len, cap_len=cap_len)


def split_heads(block):
    return block.reshape(block.shape[0], HEADS, HEAD_DIM)


def rounded(value):
    return lax.optimization_barrier(value.astype(jnp.bfloat16)).astype(jnp.float32)


def reference(video_queries, caption_keys, caption_values, out_grad, head_gate, video_len, cap_len):
    score_scale = HEAD_DIM ** -0.5
    cycle_size = N_SEQ

    def one_sample(packed):
        queries, cap_keys, values, cotangent, vid_length, cap_length = packed
        query_heads = split_heads(queries).astype(jnp.float32)
        key_heads = split_heads(cap_keys).astype(jnp.float32)
        value_heads = split_heads(values).astype(jnp.float32)
        scores = jnp.einsum("thd,jhd->htj", query_heads, key_heads) * score_scale
        key_live = jnp.arange(CAP, dtype=jnp.int32) < cap_length
        scores = jnp.where(key_live[None, None, :], scores, -jnp.inf)
        shifted = jnp.exp(scores - jnp.max(scores, axis=-1, keepdims=True))
        weights = shifted / jnp.sum(shifted, axis=-1, keepdims=True)
        weights_low = rounded(weights)
        attention = jnp.einsum("htj,jhd->thd", weights_low, value_heads)
        row_live = (jnp.arange(VIDEO, dtype=jnp.int32) < vid_length).astype(jnp.float32)[:, None, None]
        head_scale = head_gate.astype(jnp.float32)[None, :, None]
        attended = (attention * head_scale * row_live).astype(jnp.bfloat16).reshape(VIDEO, HEADS * HEAD_DIM)
        cot_heads = split_heads(cotangent).astype(jnp.float32)
        gate_term = jnp.sum(cot_heads * attention * row_live, axis=(0, 2))
        grad_attention = rounded(cot_heads * head_scale * row_live)
        grad_weights = jnp.einsum("thd,jhd->htj", grad_attention, value_heads)
        row_delta = jnp.sum(weights * grad_weights, axis=-1, keepdims=True)
        grad_scores = rounded(weights * (grad_weights - row_delta) * score_scale)
        query_grad = jnp.einsum("htj,jhd->thd", grad_scores, key_heads)
        query_grad = query_grad.astype(jnp.bfloat16).reshape(VIDEO, HEADS * HEAD_DIM)
        block_scores = grad_scores.reshape(HEADS, cycle_size, TOK_DEV, CAP)
        block_weights = weights_low.reshape(HEADS, cycle_size, TOK_DEV, CAP)
        block_queries = query_heads.reshape(cycle_size, TOK_DEV, HEADS, HEAD_DIM)
        block_grads = grad_attention.reshape(cycle_size, TOK_DEV, HEADS, HEAD_DIM)
        key_parts = rounded(jnp.einsum("hrtj,rthd->rjhd", block_scores, block_queries))
        value_parts = rounded(jnp.einsum("hrtj,rthd->rjhd", block_weights, block_grads))
        key_grad = jnp.sum(key_parts, axis=0).astype(jnp.bfloat16).reshape(CAP, HEADS * HEAD_DIM)
        value_grad = jnp.sum(value_parts, axis=0).astype(jnp.bfloat16).reshape(CAP, HEADS * HEAD_DIM)
        return attended, query_grad, key_grad, value_grad, gate_term

    per_sample = lax.map(one_sample, (video_queries, caption_keys, caption_values, out_grad, video_len, cap_len))
    return per_sample[0], per_sample[1], per_sample[2], per_sample[3], jnp.sum(per_sample[4], axis=0)
```

```python
import functools
import math

import jax
import jax.numpy as jnp
from jax import lax
from jax.experimental import pallas as pl
from jax.experimental.pallas import tpu as pltpu
from jax.sharding import Mesh
from jax.sharding import PartitionSpec as P

HALF = "z_far"
NEAR = ("z_near", "x")
DP = ("y", "z_hi")
WIDTH = 128
LIMIT = 56 * 2**20
VMEM = pl.BlockSpec(memory_space=pltpu.VMEM)
SMEM = pl.BlockSpec(memory_space=pltpu.SMEM)


def in_vmem(x):
    return pltpu.with_memory_space_constraint(x, pltpu.VMEM)


def call(kernel, outs, specs, args, scratch=(), limit=None):
    return pl.pallas_call(
        kernel,
        out_shape=tuple(
            out if isinstance(out, jax.ShapeDtypeStruct) else pltpu.VMEM(*out) for out in outs
        ),
        in_specs=specs,
        out_specs=(VMEM,) * len(outs),
        scratch_shapes=scratch,
        compiler_params=pltpu.CompilerParams(vmem_limit_bytes=limit),
    )(*args)


def pack_kernel(a_ref, b_ref, out_ref):
    rows = a_ref.shape[1]
    width = out_ref.shape[2]
    for u in range(out_ref.shape[0]):
        cols = slice(u * width, (u + 1) * width)
        out_ref[u, 0:rows, :] = a_ref[0, :, cols]
        out_ref[u, rows : 2 * rows, :] = b_ref[0, :, cols]


def unpack_kernel(in_ref, a_ref, b_ref):
    rows = a_ref.shape[1]
    width = in_ref.shape[2]
    for u in range(in_ref.shape[0]):
        cols = slice(u * width, (u + 1) * width)
        a_ref[0, :, cols] = in_ref[u, 0:rows, :]
        b_ref[0, :, cols] = in_ref[u, rows : 2 * rows, :]


def add_kernel(a_ref, b_ref, out_ref):
    total = a_ref[...].astype(jnp.float32) + b_ref[...].astype(jnp.float32)
    out_ref[...] = total.astype(jnp.bfloat16)


def contract(a, b, dims):
    return lax.dot_general(a, b, (dims, ((), ())), preferred_element_type=jnp.float32)


def load_captions(caps, far, cols, near_ref, far_ref, key_ref, value_ref):
    half = near_ref.shape[0] * caps
    for start, ref in ((far * half, near_ref), (half - far * half, far_ref)):
        place = pl.ds(pl.multiple_of(start, half), half)
        key_ref[place, :] = ref[:, 0:caps, cols].reshape(half, WIDTH)
        value_ref[place, :] = ref[:, caps:, cols].reshape(half, WIDTH)


def live_cot(info_ref, x_ref, step, cols):
    rows = x_ref.shape[1] // 2
    tile = 2 * rows
    cot = x_ref[pl.ds(step * 2, 2), rows:, cols].reshape(tile, WIDTH).astype(jnp.float32)
    row = info_ref[2] + step * tile + lax.broadcasted_iota(jnp.int32, (tile, WIDTH), 0)
    live = row < info_ref[0]
    return live, jnp.where(live, cot, 0.0)


def forward_kernel(
    caps, info_ref, gate_ref, x_ref, kvn_ref, kvf_ref, out_ref, w_ref, delta_ref, gsum_ref, *scratch
):
    bias_ref, key_ref, value_ref, vt_ref = scratch
    owners, double, columns = x_ref.shape
    rows = double // 2
    captions, tile = bias_ref.shape
    scale = WIDTH ** (-0.5)
    position = lax.broadcasted_iota(jnp.int32, (captions, tile), 0)
    bias_ref[...] = jnp.where(position < info_ref[1], 0.0, -jnp.inf)
    lane = lax.broadcasted_iota(jnp.int32, (1, WIDTH), 1)
    gate_sum = jnp.zeros((1, WIDTH), jnp.float32)
    steps = owners // 2
    for h in range(columns // WIDTH):
        cols = slice(h * WIDTH, (h + 1) * WIDTH)
        gate = gate_ref[h]
        load_captions(caps, info_ref[3], cols, kvn_ref, kvf_ref, key_ref, value_ref)
        vt_ref[...] = value_ref[...].T

        def body(step, gate_acc):
            block = pl.ds(step * 2, 2)
            queries = x_ref[block, 0:rows, cols].reshape(tile, WIDTH)
            live, cot = live_cot(info_ref, x_ref, step, cols)
            scores = contract(key_ref[...], queries, ((1,), (1,))) + bias_ref[...]
            top = jnp.max(scores, axis=0, keepdims=True)
            shifted = jnp.exp2((scores - top) * (scale * math.log2(math.e)))
            inverse = 1.0 / jnp.sum(shifted, axis=0, keepdims=True)
            weights = (shifted * inverse).astype(jnp.bfloat16)
            w_ref[h * steps + step] = weights
            attention_t = contract(vt_ref[...], weights, ((1,), (0,)))
            attention = attention_t.T
            attended = jnp.where(live, attention * gate, 0.0).astype(jnp.bfloat16)
            out_ref[block, :, cols] = attended.reshape(2, rows, WIDTH)
            grad_att_t = (cot * gate).astype(jnp.bfloat16).T
            delta_ref[h * steps + step] = jnp.sum(
                grad_att_t.astype(jnp.float32) * attention_t, axis=0, keepdims=True
            )
            return gate_acc + jnp.sum(cot * attention, axis=0, keepdims=True)

        zero = jnp.zeros((1, WIDTH), jnp.float32)
        gate_acc = lax.fori_loop(0, steps, body, zero, unroll=2)
        total = jnp.sum(gate_acc, axis=1, keepdims=True)
        gate_sum = gate_sum + jnp.where(lane == info_ref[4] + h, total, 0.0)
    gsum_ref[...] = gate_sum


def backward_kernel(
    caps, info_ref, gate_ref, x_ref, kvn_ref, kvf_ref, att_ref, w_ref, delta_ref, *rest
):
    out_ref, near_ref, far_ref, key_ref, value_ref, kt_ref, dk_ref, dv_ref = rest
    owners, double, columns = x_ref.shape
    rows = double // 2
    half = owners * caps
    tile = 2 * rows
    scale = WIDTH ** (-0.5)
    steps = owners // 2
    out_ref[:, 0:rows, :] = att_ref[...]
    for h in range(columns // WIDTH):
        cols = slice(h * WIDTH, (h + 1) * WIDTH)
        gate = gate_ref[h]
        load_captions(caps, info_ref[3], cols, kvn_ref, kvf_ref, key_ref, value_ref)
        kt_ref[...] = key_ref[...].T
        dk_ref[...] = jnp.zeros_like(dk_ref)
        dv_ref[...] = jnp.zeros_like(dv_ref)

        def body(step, carry):
            block = pl.ds(step * 2, 2)
            queries = x_ref[block, 0:rows, cols].reshape(tile, WIDTH)
            _, cot = live_cot(info_ref, x_ref, step, cols)
            grad_att = (cot * gate).astype(jnp.bfloat16)
            weights = w_ref[h * steps + step]
            grad_weights = contract(value_ref[...], grad_att, ((1,), (1,)))
            spread = grad_weights - delta_ref[h * steps + step]
            grad_scores = (weights.astype(jnp.float32) * spread).astype(jnp.bfloat16)
            query_grad = (contract(kt_ref[...], grad_scores, ((1,), (0,))) * scale).T
            out_ref[block, rows:, cols] = query_grad.astype(jnp.bfloat16).reshape(2, rows, WIDTH)
            dk_ref[...] += contract(grad_scores, queries, ((1,), (0,)))
            dv_ref[...] += contract(weights, grad_att, ((1,), (0,)))
            return carry

        lax.fori_loop(0, steps, body, 0, unroll=2)
        for start, ref in ((info_ref[3] * half, near_ref), (half - info_ref[3] * half, far_ref)):
            place = pl.ds(pl.multiple_of(start, half), half)
            key_grad = (dk_ref[place, :] * scale).astype(jnp.bfloat16)
            value_grad = dv_ref[place, :].astype(jnp.bfloat16)
            ref[:, 0:caps, cols] = key_grad.reshape(owners, caps, WIDTH)
            ref[:, caps:, cols] = value_grad.reshape(owners, caps, WIDTH)


def exchange(x):
    return lax.all_to_all(x, NEAR, split_axis=0, concat_axis=0, tiled=True)


def add_partner(x, axis, reach):
    pairs = [(i, i ^ reach) for i in range(lax.axis_size(axis))]
    return x + lax.ppermute(x, axis, pairs)


def add_group(x, axes):
    copies = jnp.broadcast_to(x, (lax.axis_size(axes), *x.shape))
    gathered = lax.all_to_all(copies, axes, split_axis=0, concat_axis=0, tiled=True)
    return jnp.sum(gathered, axis=0)


def per_device(
    video_queries, caption_keys, caption_values, out_grad, head_gate, video_len, cap_len
):
    rows, caps = video_queries.shape[1], caption_keys.shape[1]
    head_count = head_gate.shape[0]
    owners = lax.axis_size(NEAR)
    columns = video_queries.shape[2] // owners
    far = lax.axis_index(HALF)
    local_heads = columns // 128
    head = (lax.axis_index("grp") * owners + lax.axis_index(NEAR)) * local_heads
    swap = [(0, 1), (1, 0)]
    bf16, f32 = jnp.bfloat16, jnp.float32
    pair_of = lambda n: ((owners, 2 * n, columns), bf16)

    (kv_packed,) = call(pack_kernel, [pair_of(caps)], [VMEM] * 2, (caption_keys, caption_values))
    (packed,) = call(pack_kernel, [pair_of(rows)], [VMEM] * 2, (video_queries, out_grad))
    packed, kv_near = lax.optimization_barrier((packed, exchange(kv_packed)))
    kv_far = lax.ppermute(kv_near, HALF, swap)
    mine = exchange(packed)

    info = jnp.stack([video_len[0], cap_len[0], far * (owners * rows), far, head])
    gate = lax.dynamic_slice_in_dim(head_gate, head, local_heads)
    captions, tile = 2 * owners * caps, 2 * rows
    tiles = local_heads * owners // 2
    operands = (
        info.astype(jnp.int32), gate, in_vmem(mine), in_vmem(kv_near), in_vmem(kv_far)
    )
    specs = [SMEM, SMEM, VMEM, VMEM, VMEM]
    tall, wide = (captions, WIDTH), (WIDTH, captions)
    attended, weights, delta, gate_sum = call(
        functools.partial(forward_kernel, caps),
        [
            ((owners, rows, columns), bf16),
            jax.ShapeDtypeStruct((tiles, captions, tile), bf16),
            ((tiles, 1, tile), f32),
            ((1, WIDTH), f32),
        ],
        specs,
        operands,
        [
            pltpu.VMEM((captions, tile), f32),
            pltpu.VMEM(tall, bf16),
            pltpu.VMEM(tall, bf16),
            pltpu.VMEM(wide, bf16),
        ],
        LIMIT,
    )
    gate_sum = add_group(gate_sum, (HALF, *NEAR, "grp"))
    result, near, away = call(
        functools.partial(backward_kernel, caps),
        [pair_of(rows), pair_of(caps), pair_of(caps)],
        specs + [VMEM] * 3,
        operands + (in_vmem(attended), weights, in_vmem(delta)),
        [
            pltpu.VMEM(tall, bf16),
            pltpu.VMEM(tall, bf16),
            pltpu.VMEM(wide, bf16),
            pltpu.VMEM(tall, f32),
            pltpu.VMEM(tall, f32),
        ],
        LIMIT,
    )
    back = exchange(result)
    arrived = lax.ppermute(away, HALF, swap)
    gate_sum = lax.psum(gate_sum, "z_hi")
    back, near, gate_sum = lax.optimization_barrier((back, near, gate_sum))
    (both,) = call(add_kernel, [pair_of(caps)], [VMEM] * 2, (in_vmem(near), in_vmem(arrived)))
    caption_back = exchange(both)
    gate_sum = lax.psum(gate_sum, "y")

    def unpack(x, n):
        return pl.pallas_call(
            unpack_kernel,
            out_shape=(jax.ShapeDtypeStruct((1, n, owners * columns), bf16),) * 2,
            in_specs=[VMEM],
            out_specs=(VMEM,) * 2,
        )(in_vmem(x))

    attended, query_grad = unpack(back, rows)
    key_grad, value_grad = unpack(caption_back, caps)
    return attended, query_grad, key_grad, value_grad, gate_sum[0, :head_count]


def solution(mesh):
    split = Mesh(
        mesh.devices.reshape(2, 2, 4, 8, 4, mesh.shape["grp"]),
        ("z_far", "z_near", "x", "y", "z_hi", "grp"),
    )
    wide = P(DP, (HALF, *NEAR), "grp")
    return jax.shard_map(
        per_device,
        mesh=split,
        in_specs=(wide, wide, wide, wide, P(), P(DP), P(DP)),
        out_specs=(wide, wide, wide, wide, P()),
        check_vma=False,
    )
```

```python
import functools
import math

import jax
import jax.numpy as jnp
from jax import lax
from jax.experimental import pallas as pl
from jax.experimental.pallas import tpu as pltpu
from jax.sharding import Mesh
from jax.sharding import PartitionSpec as P

HALF = "z_far"
NEAR = ("z_near", "x")
DP = ("y", "z_hi")
WIDTH = 128
LIMIT = 56 * 2**20
VMEM = pl.BlockSpec(memory_space=pltpu.VMEM)
SMEM = pl.BlockSpec(memory_space=pltpu.SMEM)


def in_vmem(x):
    return pltpu.with_memory_space_constraint(x, pltpu.VMEM)


def call(kernel, outs, specs, args, scratch=(), limit=None, out_specs=None):
    return pl.pallas_call(
        kernel,
        out_shape=tuple(
            out if isinstance(out, jax.ShapeDtypeStruct) else pltpu.VMEM(*out) for out in outs
        ),
        in_specs=specs,
        out_specs=out_specs or (VMEM,) * len(outs),
        scratch_shapes=scratch,
        compiler_params=pltpu.CompilerParams(vmem_limit_bytes=limit),
    )(*args)


def pack_kernel(a_ref, b_ref, out_ref):
    rows = a_ref.shape[1]
    width = out_ref.shape[2]
    for u in range(out_ref.shape[0]):
        cols = slice(u * width, (u + 1) * width)
        out_ref[u, 0:rows, :] = a_ref[0, :, cols]
        out_ref[u, rows : 2 * rows, :] = b_ref[0, :, cols]


def unpack_kernel(in_ref, *outs):
    width = in_ref.shape[2]
    for u in range(in_ref.shape[0]):
        cols = slice(u * width, (u + 1) * width)
        row = 0
        for out_ref in outs:
            out_ref[0, :, cols] = in_ref[u, row : row + out_ref.shape[1], :]
            row += out_ref.shape[1]


def add_kernel(a_ref, b_ref, out_ref):
    total = a_ref[...].astype(jnp.float32) + b_ref[...].astype(jnp.float32)
    out_ref[...] = total.astype(jnp.bfloat16)


def contract(a, b, dims):
    return lax.dot_general(a, b, (dims, ((), ())), preferred_element_type=jnp.float32)


def load_captions(caps, far, cols, near_ref, far_ref, key_ref, value_ref):
    half = near_ref.shape[0] * caps
    for start, ref in ((far * half, near_ref), (half - far * half, far_ref)):
        place = pl.ds(pl.multiple_of(start, half), half)
        key_ref[place, :] = ref[:, 0:caps, cols].reshape(half, WIDTH)
        value_ref[place, :] = ref[:, caps:, cols].reshape(half, WIDTH)


def live_cot(info_ref, x_ref, step, cols):
    rows = x_ref.shape[1] // 2
    tile = 2 * rows
    cot = x_ref[pl.ds(step * 2, 2), rows:, cols].reshape(tile, WIDTH).astype(jnp.float32)
    row = info_ref[2] + step * tile + lax.broadcasted_iota(jnp.int32, (tile, WIDTH), 0)
    live = row < info_ref[0]
    return live, jnp.where(live, cot, 0.0)


def forward_kernel(
    caps, info_ref, gate_ref, x_ref, kvn_ref, kvf_ref, out_ref, w_ref, delta_ref, gsum_ref, *scratch
):
    bias_ref, key_ref, value_ref, vt_ref, held_ref, sems = scratch
    owners, double, columns = x_ref.shape
    rows = double // 2
    captions, tile = bias_ref.shape
    scale = WIDTH ** (-0.5)
    position = lax.broadcasted_iota(jnp.int32, (captions, tile), 0)
    bias_ref[...] = jnp.where(position < info_ref[1], 0.0, -jnp.inf)
    lane = lax.broadcasted_iota(jnp.int32, (1, WIDTH), 1)
    gate_sum = jnp.zeros((1, WIDTH), jnp.float32)
    steps = owners // 2
    for h in range(columns // WIDTH):
        cols = slice(h * WIDTH, (h + 1) * WIDTH)
        gate = gate_ref[h]
        load_captions(caps, info_ref[3], cols, kvn_ref, kvf_ref, key_ref, value_ref)
        vt_ref[...] = value_ref[...].T

        def body(step, gate_acc):
            block = pl.ds(step * 2, 2)
            queries = x_ref[block, 0:rows, cols].reshape(tile, WIDTH)
            live, cot = live_cot(info_ref, x_ref, step, cols)
            scores = contract(key_ref[...], queries, ((1,), (1,))) + bias_ref[...]
            top = jnp.max(scores, axis=0, keepdims=True)
            shifted = jnp.exp2((scores - top) * (scale * math.log2(math.e)))
            inverse = 1.0 / jnp.sum(shifted, axis=0, keepdims=True)
            weights = (shifted * inverse).astype(jnp.bfloat16)
            at = h * steps + step
            held_ref[at] = weights
            pltpu.make_async_copy(held_ref.at[at], w_ref.at[at], sems.at[at]).start()
            attention_t = contract(vt_ref[...], weights, ((1,), (0,)))
            attention = attention_t.T
            attended = jnp.where(live, attention * gate, 0.0).astype(jnp.bfloat16)
            out_ref[block, :, cols] = attended.reshape(2, rows, WIDTH)
            grad_att_t = (cot * gate).astype(jnp.bfloat16).T
            delta_ref[at] = jnp.sum(
                grad_att_t.astype(jnp.float32) * attention_t, axis=0, keepdims=True
            )
            return gate_acc + jnp.sum(cot * attention, axis=0, keepdims=True)

        zero = jnp.zeros((1, WIDTH), jnp.float32)
        gate_acc = lax.fori_loop(0, steps, body, zero, unroll=2)
        total = jnp.sum(gate_acc, axis=1, keepdims=True)
        gate_sum = gate_sum + jnp.where(lane == info_ref[4] + h, total, 0.0)
    gsum_ref[...] = gate_sum
    for at in range(held_ref.shape[0]):
        pltpu.make_async_copy(held_ref.at[at], w_ref.at[at], sems.at[at]).wait()


def backward_kernel(
    caps, info_ref, gate_ref, x_ref, kvn_ref, kvf_ref, att_ref, w_ref, delta_ref, *rest
):
    out_ref, far_ref, key_ref, value_ref, kt_ref, dk_ref, dv_ref = rest
    owners, double, columns = x_ref.shape
    rows = double // 2
    half = owners * caps
    tile = 2 * rows
    scale = WIDTH ** (-0.5)
    steps = owners // 2
    out_ref[:, 0:rows, :] = att_ref[...]
    for h in range(columns // WIDTH):
        cols = slice(h * WIDTH, (h + 1) * WIDTH)
        gate = gate_ref[h]
        load_captions(caps, info_ref[3], cols, kvn_ref, kvf_ref, key_ref, value_ref)
        kt_ref[...] = key_ref[...].T
        dk_ref[...] = jnp.zeros_like(dk_ref)
        dv_ref[...] = jnp.zeros_like(dv_ref)

        def body(step, carry):
            block = pl.ds(step * 2, 2)
            queries = x_ref[block, 0:rows, cols].reshape(tile, WIDTH)
            _, cot = live_cot(info_ref, x_ref, step, cols)
            grad_att = (cot * gate).astype(jnp.bfloat16)
            weights = w_ref[h * steps + step]
            grad_weights = contract(value_ref[...], grad_att, ((1,), (1,)))
            spread = grad_weights - delta_ref[h * steps + step]
            grad_scores = (weights.astype(jnp.float32) * spread).astype(jnp.bfloat16)
            query_grad = (contract(kt_ref[...], grad_scores, ((1,), (0,))) * scale).T
            out_ref[block, rows:double, cols] = query_grad.astype(jnp.bfloat16).reshape(2, rows, WIDTH)
            dk_ref[...] += contract(grad_scores, queries, ((1,), (0,)))
            dv_ref[...] += contract(weights, grad_att, ((1,), (0,)))
            return carry

        lax.fori_loop(0, steps, body, 0, unroll=2)
        mine = info_ref[3] * half
        for start, ref, row in ((mine, out_ref, double), (half - mine, far_ref, 0)):
            place = pl.ds(pl.multiple_of(start, half), half)
            key_grad = (dk_ref[place, :] * scale).astype(jnp.bfloat16)
            value_grad = dv_ref[place, :].astype(jnp.bfloat16)
            ref[:, row : row + caps, cols] = key_grad.reshape(owners, caps, WIDTH)
            ref[:, row + caps : row + 2 * caps, cols] = value_grad.reshape(owners, caps, WIDTH)


def exchange(x):
    return lax.all_to_all(x, NEAR, split_axis=0, concat_axis=0, tiled=True)


def add_partner(x, axis, reach):
    pairs = [(i, i ^ reach) for i in range(lax.axis_size(axis))]
    return x + lax.ppermute(x, axis, pairs)


def add_group(x, axes):
    copies = jnp.broadcast_to(x, (lax.axis_size(axes), *x.shape))
    gathered = lax.all_to_all(copies, axes, split_axis=0, concat_axis=0, tiled=True)
    return jnp.sum(gathered, axis=0)


def per_device(
    video_queries, caption_keys, caption_values, out_grad, head_gate, video_len, cap_len
):
    rows, caps = video_queries.shape[1], caption_keys.shape[1]
    head_count = head_gate.shape[0]
    owners = lax.axis_size(NEAR)
    columns = video_queries.shape[2] // owners
    far = lax.axis_index(HALF)
    local_heads = columns // 128
    head = (lax.axis_index("grp") * owners + lax.axis_index(NEAR)) * local_heads
    swap = [(0, 1), (1, 0)]
    bf16, f32 = jnp.bfloat16, jnp.float32
    pair_of = lambda n: ((owners, 2 * n, columns), bf16)

    (kv_packed,) = call(pack_kernel, [pair_of(caps)], [VMEM] * 2, (caption_keys, caption_values))
    (packed,) = call(pack_kernel, [pair_of(rows)], [VMEM] * 2, (video_queries, out_grad))
    packed, kv_near = lax.optimization_barrier((packed, exchange(kv_packed)))
    kv_far = lax.ppermute(kv_near, HALF, swap)
    mine = exchange(packed)

    info = jnp.stack([video_len[0], cap_len[0], far * (owners * rows), far, head])
    gate = lax.dynamic_slice_in_dim(head_gate, head, local_heads)
    captions, tile = 2 * owners * caps, 2 * rows
    tiles = local_heads * owners // 2
    operands = (
        info.astype(jnp.int32), gate, in_vmem(mine), in_vmem(kv_near), in_vmem(kv_far)
    )
    specs = [SMEM, SMEM, VMEM, VMEM, VMEM]
    tall, wide = (captions, WIDTH), (WIDTH, captions)
    attended, weights, delta, gate_sum = call(
        functools.partial(forward_kernel, caps),
        [
            ((owners, rows, columns), bf16),
            jax.ShapeDtypeStruct((tiles, captions, tile), bf16),
            ((tiles, 1, tile), f32),
            ((1, WIDTH), f32),
        ],
        specs,
        operands,
        [
            pltpu.VMEM((captions, tile), f32),
            pltpu.VMEM(tall, bf16),
            pltpu.VMEM(tall, bf16),
            pltpu.VMEM(wide, bf16),
            pltpu.VMEM((tiles, captions, tile), bf16),
            pltpu.SemaphoreType.DMA((tiles,)),
        ],
        LIMIT,
        (VMEM, pl.BlockSpec(memory_space=pl.ANY), VMEM, VMEM),
    )
    gate_sum = add_group(gate_sum, (HALF, *NEAR, "grp"))
    result, away = call(
        functools.partial(backward_kernel, caps),
        [jax.ShapeDtypeStruct(*pair_of(rows + caps)), pair_of(caps)],
        specs + [VMEM] * 3,
        operands + (in_vmem(attended), weights, in_vmem(delta)),
        [
            pltpu.VMEM(tall, bf16),
            pltpu.VMEM(tall, bf16),
            pltpu.VMEM(wide, bf16),
            pltpu.VMEM(tall, f32),
            pltpu.VMEM(tall, f32),
        ],
        LIMIT,
    )
    away, gate_sum = lax.optimization_barrier((away, gate_sum))
    arrived = lax.ppermute(away, HALF, swap)
    gate_sum = lax.psum(gate_sum, "z_hi")
    arrived, gate_sum = lax.optimization_barrier((arrived, gate_sum))
    block = pl.BlockSpec((owners, 2 * caps, columns), lambda i: (0, rows // caps, 0))
    joined = pl.pallas_call(
        add_kernel,
        out_shape=jax.ShapeDtypeStruct(result.shape, bf16),
        in_specs=[block, VMEM],
        out_specs=block,
        grid=(1,),
        input_output_aliases={0: 0},
    )(result, in_vmem(arrived))
    back = exchange(joined)
    gate_sum = lax.psum(gate_sum, "y")
    attended, query_grad, key_grad, value_grad = pl.pallas_call(
        unpack_kernel,
        out_shape=tuple(
            jax.ShapeDtypeStruct((1, n, owners * columns), bf16)
            for n in (rows, rows, caps, caps)
        ),
        in_specs=[VMEM],
        out_specs=(VMEM,) * 4,
    )(in_vmem(back))
    return attended, query_grad, key_grad, value_grad, gate_sum[0, :head_count]


def solution(mesh):
    split = Mesh(
        mesh.devices.reshape(2, 2, 4, 8, 4, mesh.shape["grp"]),
        ("z_far", "z_near", "x", "y", "z_hi", "grp"),
    )
    wide = P(DP, (HALF, *NEAR), "grp")
    return jax.shard_map(
        per_device,
        mesh=split,
        in_specs=(wide, wide, wide, wide, P(), P(DP), P(DP)),
        out_specs=(wide, wide, wide, wide, P()),
        check_vma=False,
    )
```

```python
import functools
import math

import jax
import jax.numpy as jnp
from jax import lax
from jax.experimental import pallas as pl
from jax.experimental.pallas import tpu as pltpu
from jax.sharding import Mesh
from jax.sharding import PartitionSpec as P

HALF = "z_far"
NEAR = ("z_near", "x")
DP = ("y", "z_hi")
WIDTH = 128
LIMIT = 56 * 2**20
VMEM = pl.BlockSpec(memory_space=pltpu.VMEM)
SMEM = pl.BlockSpec(memory_space=pltpu.SMEM)


def in_vmem(x):
    return pltpu.with_memory_space_constraint(x, pltpu.VMEM)


def call(kernel, outs, specs, args, scratch=(), limit=None, out_specs=None):
    return pl.pallas_call(
        kernel,
        out_shape=tuple(
            out if isinstance(out, jax.ShapeDtypeStruct) else pltpu.VMEM(*out) for out in outs
        ),
        in_specs=specs,
        out_specs=out_specs or (VMEM,) * len(outs),
        scratch_shapes=scratch,
        compiler_params=pltpu.CompilerParams(vmem_limit_bytes=limit),
    )(*args)


def pack_kernel(a_ref, b_ref, out_ref):
    rows = a_ref.shape[1]
    width = out_ref.shape[2]
    for u in range(out_ref.shape[0]):
        cols = slice(u * width, (u + 1) * width)
        out_ref[u, 0:rows, :] = a_ref[0, :, cols]
        out_ref[u, rows : 2 * rows, :] = b_ref[0, :, cols]


def unpack_kernel(in_ref, *outs):
    width = in_ref.shape[2]
    for u in range(in_ref.shape[0]):
        cols = slice(u * width, (u + 1) * width)
        row = 0
        for out_ref in outs:
            out_ref[0, :, cols] = in_ref[u, row : row + out_ref.shape[1], :]
            row += out_ref.shape[1]


def add_kernel(a_ref, b_ref, out_ref):
    total = a_ref[...].astype(jnp.float32) + b_ref[...].astype(jnp.float32)
    out_ref[...] = total.astype(jnp.bfloat16)


def contract(a, b, dims):
    return lax.dot_general(a, b, (dims, ((), ())), preferred_element_type=jnp.float32)


def load_captions(caps, far, cols, near_ref, far_ref, key_ref, value_ref):
    half = near_ref.shape[0] * caps
    for start, ref in ((far * half, near_ref), (half - far * half, far_ref)):
        place = pl.ds(pl.multiple_of(start, half), half)
        key_ref[place, :] = ref[:, 0:caps, cols].reshape(half, WIDTH)
        value_ref[place, :] = ref[:, caps:, cols].reshape(half, WIDTH)


def live_cot(info_ref, x_ref, step, cols):
    rows = x_ref.shape[1] // 2
    tile = 2 * rows
    cot = x_ref[pl.ds(step * 2, 2), rows:, cols].reshape(tile, WIDTH).astype(jnp.float32)
    row = info_ref[2] + step * tile + lax.broadcasted_iota(jnp.int32, (tile, WIDTH), 0)
    live = row < info_ref[0]
    return live, jnp.where(live, cot, 0.0)


def forward_kernel(
    caps, info_ref, gate_ref, x_ref, kvn_ref, kvf_ref, out_ref, w_ref, delta_ref, gsum_ref, *scratch
):
    bias_ref, key_ref, value_ref, vt_ref, held_ref, sems = scratch
    owners, double, columns = x_ref.shape
    rows = double // 2
    captions, tile = bias_ref.shape
    scale = WIDTH ** (-0.5)
    position = lax.broadcasted_iota(jnp.int32, (captions, tile), 0)
    bias_ref[...] = jnp.where(position < info_ref[1], 0.0, -jnp.inf)
    lane = lax.broadcasted_iota(jnp.int32, (1, WIDTH), 1)
    gate_sum = jnp.zeros((1, WIDTH), jnp.float32)
    steps = owners // 2
    for h in range(columns // WIDTH):
        cols = slice(h * WIDTH, (h + 1) * WIDTH)
        gate = gate_ref[h]
        load_captions(caps, info_ref[3], cols, kvn_ref, kvf_ref, key_ref, value_ref)
        vt_ref[...] = value_ref[...].T

        def body(step, gate_acc):
            block = pl.ds(step * 2, 2)
            queries = x_ref[block, 0:rows, cols].reshape(tile, WIDTH)
            live, cot = live_cot(info_ref, x_ref, step, cols)
            scores = contract(key_ref[...], queries, ((1,), (1,))) + bias_ref[...]
            top = jnp.max(scores, axis=0, keepdims=True)
            shifted = jnp.exp2((scores - top) * (scale * math.log2(math.e)))
            inverse = 1.0 / jnp.sum(shifted, axis=0, keepdims=True)
            weights = (shifted * inverse).astype(jnp.bfloat16)
            at = h * steps + step
            held_ref[at] = weights
            pltpu.make_async_copy(held_ref.at[at], w_ref.at[at], sems.at[at]).start()
            attention_t = contract(vt_ref[...], weights, ((1,), (0,)))
            attention = attention_t.T
            attended = jnp.where(live, attention * gate, 0.0).astype(jnp.bfloat16)
            out_ref[block, :, cols] = attended.reshape(2, rows, WIDTH)
            grad_att_t = (cot * gate).astype(jnp.bfloat16).T
            delta_ref[at] = jnp.sum(
                grad_att_t.astype(jnp.float32) * attention_t, axis=0, keepdims=True
            )
            return gate_acc + jnp.sum(cot * attention, axis=0, keepdims=True)

        zero = jnp.zeros((1, WIDTH), jnp.float32)
        gate_acc = lax.fori_loop(0, steps, body, zero, unroll=4)
        total = jnp.sum(gate_acc, axis=1, keepdims=True)
        gate_sum = gate_sum + jnp.where(lane == info_ref[4] + h, total, 0.0)
    gsum_ref[...] = jnp.broadcast_to(gate_sum[None], gsum_ref.shape)
    for at in range(held_ref.shape[0]):
        pltpu.make_async_copy(held_ref.at[at], w_ref.at[at], sems.at[at]).wait()


def backward_kernel(
    caps, info_ref, gate_ref, x_ref, kvn_ref, kvf_ref, att_ref, w_ref, delta_ref, *rest
):
    out_ref, far_ref, key_ref, value_ref, kt_ref, dk_ref, dv_ref = rest
    owners, double, columns = x_ref.shape
    rows = double // 2
    half = owners * caps
    tile = 2 * rows
    scale = WIDTH ** (-0.5)
    steps = owners // 2
    out_ref[:, 0:rows, :] = att_ref[...]
    for h in range(columns // WIDTH):
        cols = slice(h * WIDTH, (h + 1) * WIDTH)
        gate = gate_ref[h]
        load_captions(caps, info_ref[3], cols, kvn_ref, kvf_ref, key_ref, value_ref)
        kt_ref[...] = key_ref[...].T
        dk_ref[...] = jnp.zeros_like(dk_ref)
        dv_ref[...] = jnp.zeros_like(dv_ref)

        def body(step, carry):
            block = pl.ds(step * 2, 2)
            queries = x_ref[block, 0:rows, cols].reshape(tile, WIDTH)
            _, cot = live_cot(info_ref, x_ref, step, cols)
            grad_att = (cot * gate).astype(jnp.bfloat16)
            weights = w_ref[h * steps + step]
            grad_weights = contract(value_ref[...], grad_att, ((1,), (1,)))
            spread = grad_weights - delta_ref[h * steps + step]
            grad_scores = (weights.astype(jnp.float32) * spread).astype(jnp.bfloat16)
            query_grad = (contract(kt_ref[...], grad_scores, ((1,), (0,))) * scale).T
            out_ref[block, rows:double, cols] = query_grad.astype(jnp.bfloat16).reshape(2, rows, WIDTH)
            dk_ref[...] += contract(grad_scores, queries, ((1,), (0,)))
            dv_ref[...] += contract(weights, grad_att, ((1,), (0,)))
            return carry

        lax.fori_loop(0, steps, body, 0, unroll=2)
        mine = info_ref[3] * half
        for start, ref, row in ((mine, out_ref, double), (half - mine, far_ref, 0)):
            place = pl.ds(pl.multiple_of(start, half), half)
            key_grad = (dk_ref[place, :] * scale).astype(jnp.bfloat16)
            value_grad = dv_ref[place, :].astype(jnp.bfloat16)
            ref[:, row : row + caps, cols] = key_grad.reshape(owners, caps, WIDTH)
            ref[:, row + caps : row + 2 * caps, cols] = value_grad.reshape(owners, caps, WIDTH)


def exchange(x):
    return lax.all_to_all(x, NEAR, split_axis=0, concat_axis=0, tiled=True)


def add_partner(x, axis, reach):
    pairs = [(i, i ^ reach) for i in range(lax.axis_size(axis))]
    return x + lax.ppermute(x, axis, pairs)


def add_group(copies, axes):
    gathered = lax.all_to_all(copies, axes, split_axis=0, concat_axis=0, tiled=True)
    return jnp.sum(gathered, axis=0)


def per_device(
    video_queries, caption_keys, caption_values, out_grad, head_gate, video_len, cap_len
):
    rows, caps = video_queries.shape[1], caption_keys.shape[1]
    head_count = head_gate.shape[0]
    owners = lax.axis_size(NEAR)
    columns = video_queries.shape[2] // owners
    far = lax.axis_index(HALF)
    local_heads = columns // 128
    head = (lax.axis_index("grp") * owners + lax.axis_index(NEAR)) * local_heads
    swap = [(0, 1), (1, 0)]
    everyone = (HALF, *NEAR, "grp")
    bf16, f32 = jnp.bfloat16, jnp.float32
    pair_of = lambda n: ((owners, 2 * n, columns), bf16)

    (kv_packed,) = call(pack_kernel, [pair_of(caps)], [VMEM] * 2, (caption_keys, caption_values))
    (packed,) = call(pack_kernel, [pair_of(rows)], [VMEM] * 2, (video_queries, out_grad))
    packed, kv_near = lax.optimization_barrier((packed, exchange(kv_packed)))
    kv_far = lax.ppermute(kv_near, HALF, swap)
    mine = exchange(packed)

    info = jnp.stack([video_len[0], cap_len[0], far * (owners * rows), far, head])
    gate = lax.dynamic_slice_in_dim(head_gate, head, local_heads)
    captions, tile = 2 * owners * caps, 2 * rows
    tiles = local_heads * owners // 2
    operands = (
        info.astype(jnp.int32), gate, in_vmem(mine), in_vmem(kv_near), in_vmem(kv_far)
    )
    specs = [SMEM, SMEM, VMEM, VMEM, VMEM]
    tall, wide = (captions, WIDTH), (WIDTH, captions)
    attended, weights, delta, gate_sum = call(
        functools.partial(forward_kernel, caps),
        [
            ((owners, rows, columns), bf16),
            jax.ShapeDtypeStruct((tiles, captions, tile), bf16),
            ((tiles, 1, tile), f32),
            jax.ShapeDtypeStruct((lax.axis_size(everyone), 1, WIDTH), f32),
        ],
        specs,
        operands,
        [
            pltpu.VMEM((captions, tile), f32),
            pltpu.VMEM(tall, bf16),
            pltpu.VMEM(tall, bf16),
            pltpu.VMEM(wide, bf16),
            pltpu.VMEM((tiles, captions, tile), bf16),
            pltpu.SemaphoreType.DMA((tiles,)),
        ],
        LIMIT,
        (VMEM, pl.BlockSpec(memory_space=pl.ANY), VMEM, VMEM),
    )
    gate_sum = add_group(gate_sum, everyone)
    result, away = call(
        functools.partial(backward_kernel, caps),
        [jax.ShapeDtypeStruct(*pair_of(rows + caps)), pair_of(caps)],
        specs + [VMEM] * 3,
        operands + (in_vmem(attended), weights, in_vmem(delta)),
        [
            pltpu.VMEM(tall, bf16),
            pltpu.VMEM(tall, bf16),
            pltpu.VMEM(wide, bf16),
            pltpu.VMEM(tall, f32),
            pltpu.VMEM(tall, f32),
        ],
        LIMIT,
    )
    away, gate_sum = lax.optimization_barrier((away, gate_sum))
    arrived = lax.ppermute(away, HALF, swap)
    gate_sum = lax.psum(gate_sum, "z_hi")
    arrived, gate_sum = lax.optimization_barrier((arrived, gate_sum))
    block = pl.BlockSpec((owners, 2 * caps, columns), lambda i: (0, rows // caps, 0))
    joined = pl.pallas_call(
        add_kernel,
        out_shape=jax.ShapeDtypeStruct(result.shape, bf16),
        in_specs=[block, VMEM],
        out_specs=block,
        grid=(1,),
        input_output_aliases={0: 0},
    )(result, in_vmem(arrived))
    back = exchange(joined)
    gate_sum = lax.psum(gate_sum, "y")
    attended, query_grad, key_grad, value_grad = pl.pallas_call(
        unpack_kernel,
        out_shape=tuple(
            jax.ShapeDtypeStruct((1, n, owners * columns), bf16)
            for n in (rows, rows, caps, caps)
        ),
        in_specs=[VMEM],
        out_specs=(VMEM,) * 4,
    )(in_vmem(back))
    return attended, query_grad, key_grad, value_grad, gate_sum[0, :head_count]


def solution(mesh):
    split = Mesh(
        mesh.devices.reshape(2, 2, 4, 8, 4, mesh.shape["grp"]),
        ("z_far", "z_near", "x", "y", "z_hi", "grp"),
    )
    wide = P(DP, (HALF, *NEAR), "grp")
    return jax.shard_map(
        per_device,
        mesh=split,
        in_specs=(wide, wide, wide, wide, P(), P(DP), P(DP)),
        out_specs=(wide, wide, wide, wide, P()),
        check_vma=False,
    )
```
